32 devices in a mesh: groups: 2 (over y), clips: 4 (over z), tm: 2 (over x), chan: 2 (over core).
Axes of the slice: x: 2, y: 2, z: 4, core: 2. Of those that a mesh axis runs over, the one named last changes fastest.
Arguments:
- video: bfloat16 [4, 64, 4, 8, 128], P(('groups', 'tm'), 'clips', None, None, 'chan'), parts along dimension 0, may hold values from -6 to 6, as said below
- frame_owner: int32 [4, 64, 1], P(('groups', 'tm'), 'clips'), parts along dimension 0, may hold values from 0 to 3, as said below
- conv_first: bfloat16 [3, 3, 3, 128, 128], replicated, may hold values from -0.109375 to 0.109375
- conv_second: bfloat16 [3, 3, 3, 128, 128], replicated, may hold values from -0.109375 to 0.109375
Outputs:
- encoded: bfloat16 [4, 128, 4, 8, 128], P(('groups', 'tm'), 'clips', None, None, 'chan'), parts along dimension 0
The draws below stay inside these ranges and needn't reach their ends.
There are 2 independent parts, one for each index of `groups`. The reference program is written for one: setup_inputs(seed, part) draws one part's arguments, and reference() takes and returns one part's arrays. A program takes and returns all parts, laid end to end along the dimension named above; an argument that names none is the same for every part. Nothing has to cross between parts.
Inputs may be any that keep to these rules, and one draw needn't show every extreme that they name: `frame_owner`: in each aligned block of 16 rows (the frames of one reader device in one period) no owner is named more than 8 times, and in every block some owner exactly 8 times. A clip may have no frame, or a single frame, in a whole period, and may have no frame over several periods in a row. `video`: A stored frame may be black: all its entries zero.
All inputs are finite; a program needn't handle non-finite values.
Results may differ from the reference program's by a relative error of at most 0.0044.
Values may be sent and summed in bfloat16 or wider, within the bound.
No kernel may reach another device: no remote copies, remote signals or barrier semaphores. Data moves between devices by JAX's collectives and lax.ppermute only.
A program may use at most 64 MiB of HBM per device.

```python
import jax
import jax.numpy as jnp
from jax import lax

C = 128
KT = 3
KS = 3
TILE_H = 4
TILE_W = 8
SLOTS = 16
CAP = 8
N_CLIPS = 4
N_TM = 2


def draw_video(key, part):
    keys = jax.random.split(key, 3)
    row_total = N_CLIPS * SLOTS
    full_shape = (N_TM, row_total, TILE_H, TILE_W, C)
    values = jnp.clip(jax.random.normal(keys[0], full_shape), -6.0, 6.0)
    black_rows = jax.random.randint(keys[2], (N_TM, 2), 0, row_total).astype(jnp.int32)
    row_ids = jnp.arange(row_total, dtype=jnp.int32)
    is_black = (row_ids[None, :] == black_rows[:, 0:1]) | (row_ids[None, :] == black_rows[:, 1:2])
    values = jnp.where(is_black[:, :, None, None, None], 0.0, values)
    return values.astype(jnp.float32).astype(jnp.bfloat16)


def draw_frame_owner(key, part):
    block_count = N_TM * N_CLIPS
    ticket_count = N_CLIPS * CAP
    keys = jax.random.split(key, 9)
    silent_clip = jax.random.randint(keys[7], (), 0, N_CLIPS).astype(jnp.int32)
    periods = jnp.arange(N_TM, dtype=jnp.int32)
    middle = (periods >= 1) & (periods <= N_TM - 2)
    other_absent = ((silent_clip + 1 + jax.random.randint(keys[0], (N_TM,), 0, N_CLIPS - 1)) % N_CLIPS).astype(jnp.int32)
    absent = jnp.where(middle, silent_clip, other_absent).astype(jnp.int32)
    single = ((absent + 1 + jax.random.randint(keys[1], (N_TM,), 0, N_CLIPS - 1)) % N_CLIPS).astype(jnp.int32)
    single_reader = jax.random.randint(keys[2], (N_TM,), 0, N_CLIPS).astype(jnp.int32)
    rank_draw = jax.random.randint(keys[3], (N_TM, N_CLIPS), 0, 1 << 20)
    owner_rank = jnp.argsort(jnp.argsort(rank_draw, axis=1, stable=True), axis=1, stable=True)
    weight = (256 // (1 + owner_rank)).astype(jnp.int32)
    block_ids = jnp.arange(block_count, dtype=jnp.int32)
    period_of = block_ids // N_CLIPS
    reader_of = block_ids % N_CLIPS
    owner_ids = jnp.arange(N_CLIPS, dtype=jnp.int32)
    qualified_mask = (owner_ids[None, :] != absent[period_of][:, None]) & (owner_ids[None, :] != single[period_of][:, None])
    block_weight = weight[period_of]
    level = jax.random.randint(keys[4], (block_count, N_CLIPS), 0, 256).astype(jnp.int32) * block_weight
    level = jnp.where(qualified_mask, level, -1)
    loaded_owner = jnp.argsort(-level, axis=1, stable=True)[:, 0].astype(jnp.int32)
    forced_reader = jax.random.randint(keys[8], (N_TM,), 0, N_CLIPS).astype(jnp.int32)
    force_block = jnp.logical_not(middle[period_of]) & (reader_of == forced_reader[period_of]) & (single[period_of] != silent_clip)
    loaded_owner = jnp.where(force_block, silent_clip, loaded_owner).astype(jnp.int32)
    voucher_holder = jnp.arange(ticket_count, dtype=jnp.int32) // CAP
    starting_offset = jax.random.randint(keys[5], (block_count, ticket_count), 0, 256).astype(jnp.int32) * block_weight[:, voucher_holder]
    extra_credit = jnp.where(voucher_holder[None, :] == loaded_owner[:, None], 1 << 20, 0)
    owner_rating = jnp.where(qualified_mask[:, voucher_holder], starting_offset + extra_credit, -1)
    order = jnp.argsort(-owner_rating, axis=1, stable=True)
    chosen = voucher_holder[order[:, :SLOTS]].astype(jnp.int32)
    is_single = reader_of == single_reader[period_of]
    last_owner = jnp.where(is_single, single[period_of], chosen[:, SLOTS - 1]).astype(jnp.int32)
    chosen = chosen.at[:, SLOTS - 1].set(last_owner)
    shuffle = jnp.argsort(jax.random.randint(keys[6], (block_count, SLOTS), 0, 1 << 20), axis=1, stable=True)
    placed = jnp.take_along_axis(chosen, shuffle, axis=1)
    return placed.reshape(N_TM, N_CLIPS * SLOTS, 1).astype(jnp.int32)


def scatter_about(rng, shape, scale, limit, kind=jnp.bfloat16):
    return jnp.clip(scale * jax.random.normal(rng, shape, jnp.float32), -limit, limit).astype(kind)


def setup_inputs(seed: int = 0, part: int = 0) -> dict:
    key_list = jax.random.split(jax.random.key(seed), 5)
    own_keys = jax.random.split(jax.random.fold_in(key_list[4], part), 5)
    return {
        "video": draw_video(jax.random.fold_in(jax.random.fold_in(key_list[4], part), 71), part),
        "frame_owner": draw_frame_owner(jax.random.fold_in(jax.random.fold_in(key_list[4], part), 71), part),
        "conv_first": scatter_about(key_list[2], (KT, KS, KS, C, C), (KT * KS * KS * C) ** -0.5, 0.109375),
        "conv_second": scatter_about(key_list[3], (KT, KS, KS, C, C), (KT * KS * KS * C) ** -0.5, 0.109375),
    }


EPSILON = 1e-06

def normalize(values):
    values = values.astype(jnp.float32)
    meansq = lax.optimization_barrier(jnp.mean(values * values, axis=-1, keepdims=True))
    return jax.nn.silu(values * lax.rsqrt(meansq + EPSILON))

def delayed(values, lag_rows, keep_mask):
    shifted = jnp.concatenate([jnp.zeros_like(values[:lag_rows]), values[:-lag_rows]], axis=0)
    return jnp.where(keep_mask[:, None, None, None], shifted, jnp.zeros_like(shifted))

def causal_conv(current, earlier, earliest, weights):
    stacked = jnp.concatenate([current, earlier, earliest], axis=-1).astype(jnp.float32)
    kernel = jnp.concatenate([weights[0], weights[1], weights[2]], axis=2).astype(jnp.float32)
    return lax.conv_general_dilated(stacked, kernel, (1, 1), 'SAME', dimension_numbers=('NHWC', 'HWIO', 'NHWC'))

def reference(video, frame_owner, conv_first, conv_second):
    rows_all = N_TM * N_CLIPS * SLOTS
    owners = frame_owner.reshape(rows_all).astype(jnp.int32)
    flat_video = video.reshape(rows_all, TILE_H, TILE_W, C)
    sequence = jnp.argsort(owners, stable=True).astype(jnp.int32)
    sorted_owner = owners[sequence]
    frames = flat_video[sequence]
    same_one = jnp.concatenate([jnp.zeros((1,), jnp.bool_), sorted_owner[1:] == sorted_owner[:-1]])
    same_two = jnp.concatenate([jnp.zeros((2,), jnp.bool_), sorted_owner[2:] == sorted_owner[:-2]])
    active = normalize(frames).astype(jnp.bfloat16)
    hidden = causal_conv(active, delayed(active, 1, same_one), delayed(active, 2, same_two), conv_first).astype(jnp.bfloat16)
    second = normalize(hidden).astype(jnp.bfloat16)
    update = causal_conv(second, delayed(second, 1, same_one), delayed(second, 2, same_two), conv_second)
    result = (frames.astype(jnp.float32) + update).astype(jnp.bfloat16)
    blocks = owners.reshape(N_TM * N_CLIPS, SLOTS)
    onehot = (blocks[:, :, None] == jnp.arange(N_CLIPS, dtype=jnp.int32)[None, None, :]).astype(jnp.int32)
    rank_table = jnp.cumsum(onehot, axis=1) - 1
    slot_rank = lax.optimization_barrier(jnp.sum(rank_table * onehot, axis=2)).reshape(rows_all)
    row_ids = jnp.arange(rows_all, dtype=jnp.int32)
    period = row_ids // (N_CLIPS * SLOTS)
    reader = row_ids // SLOTS % N_CLIPS
    target = period * (N_CLIPS * N_CLIPS * CAP) + owners * (N_CLIPS * CAP) + reader * CAP + slot_rank
    placed = jnp.zeros((N_TM * N_CLIPS * N_CLIPS * CAP, TILE_H, TILE_W, C), result.dtype)
    placed = placed.at[target[sequence]].set(result)
    return placed.reshape(N_TM, N_CLIPS * N_CLIPS * CAP, TILE_H, TILE_W, C)
```

```python
import functools

import jax
import jax.numpy as jnp
from jax import lax
from jax.experimental import pallas as pl
from jax.experimental.pallas import tpu as pltpu
from jax.sharding import PartitionSpec as P

EPSILON = 1e-06
EMPTY = 64.0
FILLED = 32.0
TAPS = 3
BACK = TAPS - 1
HALO = 2 * BACK
VMEM = pl.BlockSpec(memory_space=pltpu.VMEM)
SMEM = pl.BlockSpec(memory_space=pltpu.SMEM)


def pairing(count):
    if count & (count - 1) == 0:
        return [[i ^ d for i in range(count)] for d in range(count)]
    return [[(d - i) % count for i in range(count)] for d in range(count)]


def partner_round(me, other, count):
    if count & (count - 1) == 0:
        return me ^ other
    return lax.rem(me + other, count)


def pack_kernel(count, capacity, owner_ref, video_ref, *rest):
    outs, (slots, used) = rest[:count], rest[count:]
    me = lax.axis_index("clips")
    first_core = lax.axis_index("chan") == 0
    frames, rows, width, channels = video_ref.shape
    half = rows // 2
    slots[...] = jnp.full(slots.shape, EMPTY, slots.dtype)
    for o in range(count):
        used[o] = 0
    for s in range(frames):
        o = owner_ref[s]
        k = used[o]
        used[o] = k + 1
        upper = video_ref[s, :half].reshape(half * width, channels)
        lower = video_ref[s, half:].reshape(half * width, channels)
        left = jnp.where(first_core, upper, lower)
        right = jnp.where(first_core, lower, upper)
        slots[partner_round(me, o, count), k] = jnp.concatenate([left, right], axis=1)
    for d in range(count):
        outs[d][...] = slots[d]


def half_weights_kernel(raw_ref, out_ref):
    first_core = lax.axis_index("chan") == 0
    channels = raw_ref.shape[2]
    half = channels // 2

    def mine(t):
        full = raw_ref[t].astype(jnp.float32)
        return jnp.where(first_core, full[:, :half], full[:, half:])

    ahead = jnp.concatenate([mine(0), mine(2)], axis=1)
    behind = mine(1)
    out_ref[:, :channels] = ahead.astype(out_ref.dtype)
    out_ref[:, channels:] = jnp.concatenate([behind, behind], axis=1).astype(out_ref.dtype)


def filled(block, k):
    return (block[k, :8, :].astype(jnp.float32) < FILLED).astype(jnp.int32)


def live_in(block, capacity):
    total = filled(block, 0)
    for k in range(1, capacity):
        total = total + filled(block, k)
    return jnp.max(total)


def starts_of(lives, count):
    me = lax.axis_index("clips")
    reader = [partner_round(me, d, count) for d in range(count)]
    starts = []
    for d in range(count):
        start = jnp.int32(0)
        for e in range(count):
            if e != d:
                start = start + jnp.where(reader[e] < reader[d], lives[e], 0)
        starts.append(start)
    total = lives[0]
    for e in range(1, count):
        total = total + lives[e]
    return reader, starts, total


def tail_kernel(count, capacity, *rest):
    mine, other = rest[:count], rest[count : 2 * count]
    out_ref, mine_seq, other_seq = rest[2 * count :]
    lives = [live_in(mine[d], capacity) for d in range(count)]
    _, starts, total = starts_of(lives, count)
    dump = HALO + count * capacity
    for i in range(HALO):
        mine_seq[i] = jnp.full(mine_seq.shape[1:], EMPTY, mine_seq.dtype)
        other_seq[i] = jnp.full(mine_seq.shape[1:], EMPTY, mine_seq.dtype)
    for d in range(count):
        for k in range(capacity):
            place = jnp.where(k < lives[d], HALO + starts[d] + k, dump)
            mine_seq[place] = mine[d][k]
            other_seq[place] = other[d][k]
    for k in range(HALO):
        out_ref[0, k] = mine_seq[total + k]
        out_ref[1, k] = other_seq[total + k]


def activate(values):
    meansq = jnp.mean(values * values, axis=-1, keepdims=True)
    scaled = values * lax.rsqrt(meansq + EPSILON)
    return scaled / (1.0 + jnp.exp(-scaled))


def store_taps(planes_ref, row, values, width):
    channels = values.shape[1]
    count = values.shape[0]
    column = lax.rem(lax.broadcasted_iota(jnp.int32, values.shape, 0), width)
    before = jnp.where(column == 0, 0.0, pltpu.roll(values, 1, 0))
    after = jnp.where(column == width - 1, 0.0, pltpu.roll(values, count - 1, 0))
    for tap, plane in enumerate((before, values, after)):
        at = (row * TAPS + tap) * channels
        planes_ref[:, at : at + channels] = plane.astype(planes_ref.dtype)


def row_window(row, rows, depth):
    low, high = max(row - 1, 0), min(row + 2, rows)
    shift = low - (row - 1)
    return slice(low * depth, high * depth), slice(shift * depth, (shift + high - low) * depth)


def main_kernel(count, capacity, periods, *rest):
    mine, other = rest[:count], rest[count : 2 * count]
    tails_ref, first_ref, second_ref, out_ref, mine_seq, other_seq, planes, planes2, result = rest[
        2 * count :
    ]
    first_core = lax.axis_index("chan") == 0
    period = lax.axis_index("tm")
    slots = count * capacity
    total_frames = HALO + slots
    dump = total_frames
    _, rows, width, half = out_ref.shape
    upper = rows // 2
    channels = 2 * half

    lives = [live_in(mine[d], capacity) for d in range(count)]
    reader, starts, _ = starts_of(lives, count)
    mine_seq[...] = jnp.zeros(mine_seq.shape, mine_seq.dtype)
    other_seq[...] = jnp.zeros(other_seq.shape, other_seq.dtype)
    later = jnp.int32(0)
    for q in reversed(range(periods - 1)):
        kept = [jnp.max(filled(tails_ref.at[q, 0], k)) for k in range(HALO)]
        live = kept[0]
        for k in range(1, HALO):
            live = live + kept[k]
        live = jnp.where(q < period, live, 0)
        later = later + live
        for k in range(HALO):
            at = HALO - later + (k - (HALO - live))
            place = jnp.where((k >= HALO - live) & (at >= 0), at, dump)
            mine_seq[place] = tails_ref[q, 0, k]
            other_seq[place] = tails_ref[q, 1, k]
    for d in range(count):
        for k in range(capacity):
            place = jnp.where(k < lives[d], HALO + starts[d] + k, dump)
            mine_seq[place] = mine[d][k]
            other_seq[place] = other[d][k]

    own = mine_seq[:total_frames].astype(jnp.float32)
    far = other_seq[:total_frames].astype(jnp.float32)
    lane_low = lax.broadcasted_iota(jnp.int32, own.shape, 2) < half
    front = jnp.where(first_core, own, far)
    back = jnp.where(first_core, far, own)
    tops = jnp.where(lane_low, front, back).reshape(total_frames, upper, width, channels)
    bottoms = jnp.where(lane_low, back, front).reshape(total_frames * upper * width, channels)
    bottoms = pltpu.roll(bottoms, half, 1).reshape(total_frames, upper, width, channels)
    for row in range(rows):
        frame_row = tops[:, row] if row < upper else bottoms[:, row - upper]
        frame_row = frame_row.reshape(total_frames * width, channels)
        store_taps(planes, row, activate(frame_row), width)

    depth = TAPS * channels
    kept = total_frames - BACK
    for row in range(rows):
        lanes, taps = row_window(row, rows, depth)
        seen = planes[:, lanes]
        hidden = None
        for t in range(TAPS):
            part = jnp.dot(seen, first_ref[t, taps], preferred_element_type=jnp.float32)
            part = part[(BACK - t) * width : (BACK - t + kept) * width]
            hidden = part if hidden is None else hidden + part
        hidden = hidden.astype(jnp.bfloat16).astype(jnp.float32)
        store_taps(planes2, row, activate(hidden), width)

    frames = mine_seq[HALO:total_frames].astype(jnp.float32)
    frames = frames.reshape(slots, upper, width, channels)
    for row in range(rows):
        lanes, taps = row_window(row, rows, depth)
        part = jnp.dot(planes2[:, lanes], second_ref[taps], preferred_element_type=jnp.float32)
        now = part[BACK * width :, :half]
        previous = part[width : (1 + slots) * width, channels : channels + half]
        oldest = part[: slots * width, half:channels]
        update = now + previous + oldest
        on_low = (row < upper) == first_core
        frame_row = frames[:, row % upper].reshape(slots * width, channels)
        frame_row = jnp.where(on_low, frame_row[:, :half], frame_row[:, half:])
        result[:slots, row] = (frame_row + update).astype(result.dtype).reshape(slots, width, half)

    result[slots:] = jnp.zeros((capacity,) + result.shape[1:], result.dtype)
    for d in range(count):
        for k in range(capacity):
            value = result[jnp.where(k < lives[d], starts[d] + k, slots)]
            out_ref[reader[d] * capacity + k] = value


def call(kernel, out_shape, specs, scratch=(), flops=0, moved=0, name=None):
    many = isinstance(out_shape, (list, tuple))
    return pl.pallas_call(
        kernel,
        out_shape=out_shape,
        in_specs=specs,
        out_specs=[VMEM] * len(out_shape) if many else VMEM,
        scratch_shapes=list(scratch),
        cost_estimate=pl.CostEstimate(flops=flops, bytes_accessed=moved, transcendentals=0),
        name=name,
    )


def body(video, frame_owner, conv_first, conv_second):
    count = lax.axis_size("clips")
    periods = lax.axis_size("tm")
    local = video[0]
    slot_total, rows, width, half = local.shape
    capacity = max(2, 2 * slot_total // count)
    slots = count * capacity
    channels = 2 * half
    tile = (rows // 2 * width, channels)
    bf16 = jnp.bfloat16
    block = jax.ShapeDtypeStruct((capacity,) + tile, bf16)
    depth = TAPS * TAPS * channels

    packed = call(
        functools.partial(pack_kernel, count, capacity),
        [block] * count,
        [SMEM, VMEM],
        [pltpu.VMEM((count, capacity) + tile, bf16), pltpu.SMEM((count,), jnp.int32)],
        flops=1000000,
        moved=slots * half * rows * width * 4,
        name="pack",
    )(frame_owner[0, :, 0], local)
    rounds = pairing(count)
    mine = [packed[0]] + [None] * (count - 1)
    for d in reversed(range(1, count)):
        mine[d] = lax.ppermute(packed[d], "clips", [(i, rounds[d][i]) for i in range(count)])
    first = conv_first.reshape(TAPS, depth, channels)
    second = call(
        half_weights_kernel,
        jax.ShapeDtypeStruct((depth, 2 * channels), bf16),
        [VMEM],
        moved=5 * depth * channels * 2,
        name="half_weights",
    )(conv_second.reshape(TAPS, depth, channels))

    other = [lax.ppermute(mine[d], "chan", [(0, 1), (1, 0)]) for d in range(count)]
    sequence = pltpu.VMEM((HALO + slots + 1,) + tile, bf16)
    tail = call(
        functools.partial(tail_kernel, count, capacity),
        jax.ShapeDtypeStruct((2, HALO) + tile, bf16),
        [VMEM] * (2 * count),
        [sequence, sequence],
        moved=slots * tile[0] * channels * 8,
        name="tail",
    )(*mine, *other)
    if periods == 2:
        tails = lax.ppermute(tail, "tm", [(0, 1), (1, 0)])[None]
    else:
        tails = lax.all_gather(tail, "tm")
    frames = HALO + slots
    out = call(
        functools.partial(main_kernel, count, capacity, periods),
        jax.ShapeDtypeStruct((slots, rows, width, half), bf16),
        [VMEM] * (2 * count + 3),
        [
            sequence,
            sequence,
            pltpu.VMEM((frames * width, rows * TAPS * channels), bf16),
            pltpu.VMEM(((frames - BACK) * width, rows * TAPS * channels), bf16),
            pltpu.VMEM((slots + capacity, rows, width, half), bf16),
        ],
        flops=2 * frames * rows * width * depth * TAPS * channels * 2,
        moved=slots * tile[0] * channels * 8,
        name="resblock",
    )(*mine, *other, tails, first, second)
    return out[None]


def solution(mesh):
    placed = (
        P(("groups", "tm"), "clips", None, None, "chan"),
        P(("groups", "tm"), "clips", None),
        P(),
        P(),
    )
    return jax.shard_map(
        body,
        mesh=mesh,
        in_specs=placed,
        out_specs=P(("groups", "tm"), "clips", None, None, "chan"),
        check_vma=False,
    )
```

```python
import functools

import jax
import jax.numpy as jnp
from jax import lax
from jax.experimental import pallas as pl
from jax.experimental.pallas import tpu as pltpu
from jax.sharding import PartitionSpec as P


EPSILON = 1e-06
EMPTY = 64.0
FILLED = 32.0
TAPS = 3
BACK = TAPS - 1
HALO = 2 * BACK
PIECES = 2
ROUNDS = (3, 2, 1)
VMEM = pl.BlockSpec(memory_space=pltpu.VMEM)
SMEM = pl.BlockSpec(memory_space=pltpu.SMEM)


def pairing(count):
    if count & (count - 1) == 0:
        return [[i ^ d for i in range(count)] for d in range(count)]
    return [[(d - i) % count for i in range(count)] for d in range(count)]


def partner_round(me, other, count):
    if count & (count - 1) == 0:
        return me ^ other
    return lax.rem(me + other, count)


def pack_kernel(count, owner_hbm, video_hbm, first_hbm, second_hbm, *rest):
    outs, (first_ref, second_ref, owner_ref, video_ref, slots, sems) = rest[:count], rest[count:]
    frames, rows, width, channels = video_ref.shape
    piece = frames // PIECES
    owner_copy = pltpu.make_async_copy(owner_hbm, owner_ref, sems.at[PIECES])
    owner_copy.start()
    video_copies = []
    for i in range(PIECES):
        at = slice(i * piece, (i + 1) * piece)
        video_copies.append(
            pltpu.make_async_copy(video_hbm.at[at], video_ref.at[at], sems.at[i])
        )
        video_copies[i].start()
    weight_copies = [
        pltpu.make_async_copy(first_hbm, first_ref, sems.at[PIECES + 1]),
        pltpu.make_async_copy(second_hbm, second_ref, sems.at[PIECES + 2]),
    ]
    for copy in weight_copies:
        copy.start()
    me = lax.axis_index("clips")
    first_core = lax.axis_index("chan") == 0
    half = rows // 2
    slots[...] = jnp.full(slots.shape, EMPTY, slots.dtype)
    owner_copy.wait()
    bits = 32 // count
    used = jnp.int32(0)
    for s in range(frames):
        if s % piece == 0:
            video_copies[s // piece].wait()
        o = owner_ref[s]
        k = lax.shift_right_logical(used, o * bits) & (2**bits - 1)
        used = used + lax.shift_left(jnp.int32(1), o * bits)
        upper = video_ref[s, :half].reshape(half * width, channels)
        lower = video_ref[s, half:].reshape(half * width, channels)
        left = jnp.where(first_core, upper, lower)
        right = jnp.where(first_core, lower, upper)
        slots[partner_round(me, o, count), k] = jnp.concatenate([left, right], axis=1)
    for d in range(count):
        outs[d][...] = slots[d]
    for copy in weight_copies:
        copy.wait()


def half_weights_kernel(raw_ref, out_ref):
    first_core = lax.axis_index("chan") == 0
    channels = raw_ref.shape[2]
    half = channels // 2

    def mine(t):
        full = raw_ref[t].astype(jnp.float32)
        return jnp.where(first_core, full[:, :half], full[:, half:])

    ahead = jnp.concatenate([mine(0), mine(2)], axis=1)
    behind = mine(1)
    out_ref[:, :channels] = ahead.astype(out_ref.dtype)
    out_ref[:, channels:] = jnp.concatenate([behind, behind], axis=1).astype(out_ref.dtype)


def filled(block, k):
    return (block[k, :8, :].astype(jnp.float32) < FILLED).astype(jnp.int32)


def live_in(block, capacity):
    total = filled(block, 0)
    for k in range(1, capacity):
        total = total + filled(block, k)
    return jnp.max(total)


def starts_of(lives, count):
    me = lax.axis_index("clips")
    reader = [partner_round(me, d, count) for d in range(count)]
    starts = []
    for d in range(count):
        start = jnp.int32(0)
        for e in range(count):
            if e != d:
                start = start + jnp.where(reader[e] < reader[d], lives[e], 0)
        starts.append(start)
    total = lives[0]
    for e in range(1, count):
        total = total + lives[e]
    return reader, starts, total


def tail_kernel(count, capacity, *rest):
    mine, other = rest[:count], rest[count : 2 * count]
    out_ref, mine_seq, other_seq = rest[2 * count :]
    lives = [live_in(mine[d], capacity) for d in range(count)]
    _, starts, total = starts_of(lives, count)
    dump = HALO + count * capacity
    for i in range(HALO):
        mine_seq[i] = jnp.full(mine_seq.shape[1:], EMPTY, mine_seq.dtype)
        other_seq[i] = jnp.full(mine_seq.shape[1:], EMPTY, mine_seq.dtype)
    for d in range(count):
        for k in range(capacity):
            place = jnp.where(k < lives[d], HALO + starts[d] + k, dump)
            mine_seq[place] = mine[d][k]
            other_seq[place] = other[d][k]
    for k in range(HALO):
        out_ref[0, k] = mine_seq[total + k]
        out_ref[1, k] = other_seq[total + k]


def activate(values):
    meansq = jnp.mean(values * values, axis=-1, keepdims=True)
    scaled = values * lax.rsqrt(meansq + EPSILON)
    return scaled / (1.0 + jnp.exp(-scaled))


def join_halves(mine, other, first_core):
    frames, tall, channels = mine.shape
    half = channels // 2
    width = 8
    upper = tall // width
    lane_low = lax.broadcasted_iota(jnp.int32, mine.shape, 2) < half
    front = jnp.where(first_core, mine, other)
    back = jnp.where(first_core, other, mine)
    tops = jnp.where(lane_low, front, back).reshape(frames, upper, width, channels)
    bottoms = jnp.where(lane_low, back, front).reshape(frames * tall, channels)
    bottoms = pltpu.roll(bottoms, half, 1).reshape(frames, upper, width, channels)
    return [tops[:, i] for i in range(upper)] + [bottoms[:, i] for i in range(upper)]


def tap_planes(values, width):
    count = values.shape[0]
    column = lax.rem(lax.broadcasted_iota(jnp.int32, values.shape, 0), width)
    before = jnp.where(column == 0, 0.0, pltpu.roll(values, 1, 0))
    after = jnp.where(column == width - 1, 0.0, pltpu.roll(values, count - 1, 0))
    return jnp.concatenate([before, values, after], axis=1).astype(jnp.bfloat16)


def convolve(planes, weights):
    rows = len(planes)
    count = planes[0].shape[0]
    zero = jnp.zeros_like(planes[0])
    padded = [zero] + planes + [zero]
    stacked = jnp.concatenate(
        [jnp.concatenate(padded[row : row + TAPS], axis=1) for row in range(rows)], axis=0
    )
    out = jnp.dot(stacked, weights, preferred_element_type=jnp.float32)
    return [out[row * count : (row + 1) * count] for row in range(rows)]


def first_parts(mine, other, weights_ref, first_core, width):
    frames = mine.shape[0]
    values = join_halves(mine, other, first_core)
    channels = values[0].shape[2]
    planes = [
        tap_planes(activate(v.reshape(frames * width, channels)), width) for v in values
    ]
    weights = jnp.concatenate([weights_ref[t] for t in range(TAPS)], axis=1)
    return convolve(planes, weights)


def first_kernel(width, mine_ref, other_ref, weights_ref, out_ref):
    frames = mine_ref.shape[0]
    first_core = lax.axis_index("chan") == 0
    parts = first_parts(
        mine_ref[...].astype(jnp.float32),
        other_ref[...].astype(jnp.float32),
        weights_ref,
        first_core,
        width,
    )
    for row, part in enumerate(parts):
        out_ref[:, row] = part.reshape(frames, width, part.shape[1])


def earlier_frames(tails_ref, period, periods, scratch):
    if periods == 2:
        both = tails_ref[0].astype(jnp.float32)
        both = jnp.where((both < FILLED) & (period > 0), both, 0.0)
        return both[0], both[1]
    scratch[...] = jnp.zeros(scratch.shape, scratch.dtype)
    later = jnp.int32(0)
    for q in reversed(range(periods - 1)):
        live = jnp.max(filled(tails_ref.at[q, 0], 0))
        for k in range(1, HALO):
            live = live + jnp.max(filled(tails_ref.at[q, 0], k))
        live = jnp.where(q < period, live, 0)
        later = later + live
        for k in range(HALO):
            at = live - later + k
            place = jnp.where((k >= HALO - live) & (at >= 0), at, HALO)
            scratch[0, place] = tails_ref[q, 0, k]
            scratch[1, place] = tails_ref[q, 1, k]
    both = scratch[:, :HALO].astype(jnp.float32)
    return both[0], both[1]


def second_planes(hidden, width):
    frames, _, channels = hidden.shape
    hidden = hidden.reshape(frames * width, channels).astype(jnp.bfloat16).astype(jnp.float32)
    return tap_planes(activate(hidden), width)


def middle_kernel(count, capacity, fresh, *rest):
    mine, rest = rest[:count], rest[count:]
    other, rest = rest[: len(fresh)], rest[len(fresh) :]
    ready = [d for d in range(count) if d not in fresh]
    parts, rest = dict(zip(ready, rest[: len(ready)])), rest[len(ready) :]
    first_ref, second_ref, update_ref, head_ref, sequence = rest
    first_core = lax.axis_index("chan") == 0
    slots = count * capacity
    _, rows, width, half = update_ref.shape
    channels = 2 * half

    lives = [live_in(mine[d], capacity) for d in range(count)]
    _, starts, _ = starts_of(lives, count)

    def place(d, k):
        return jnp.where(k < lives[d], starts[d] + k, slots)

    for d in ready:
        for k in range(capacity):
            sequence[place(d, k)] = parts[d][k]
    own = jnp.concatenate([mine[d][...] for d in fresh], axis=0).astype(jnp.float32)
    far = jnp.concatenate([block[...] for block in other], axis=0).astype(jnp.float32)
    for row, part in enumerate(first_parts(own, far, first_ref, first_core, width)):
        part = part.reshape(len(fresh) * capacity, width, part.shape[1])
        for i, d in enumerate(fresh):
            for k in range(capacity):
                sequence[place(d, k), row] = part[i * capacity + k]

    planes = []
    for row in range(rows):
        hidden = sequence[BACK:slots, row, :, :channels]
        for t in range(1, TAPS):
            lanes = slice(t * channels, (t + 1) * channels)
            hidden = hidden + sequence[BACK - t : slots - t, row, :, lanes]
        planes.append(second_planes(hidden, width))
        head_ref[0, row] = sequence[0, row, :, :channels]
        head_ref[1, row] = (
            sequence[1, row, :, :channels] + sequence[0, row, :, channels : 2 * channels]
        )
    zero = jnp.zeros((width, half), jnp.float32)
    for row, part in enumerate(convolve(planes, second_ref[...])):
        now = part[:, :half]
        previous = jnp.concatenate([zero, part[:-width, channels : channels + half]], axis=0)
        oldest = jnp.concatenate([zero, zero, part[: -2 * width, half:channels]], axis=0)
        update_ref[BACK:slots, row] = (now + previous + oldest).reshape(-1, width, half)
        for i in range(BACK):
            update_ref[i, row] = zero


def last_kernel(count, capacity, periods, *rest):
    mine, rest = rest[:count], rest[count:]
    update_ref, head_ref, tails_ref, first_ref, second_ref, out_hbm, early, extra, out_ref, sems = rest
    first_core = lax.axis_index("chan") == 0
    period = lax.axis_index("tm")
    _, rows, width, half = out_ref.shape
    upper = rows // 2
    channels = 2 * half

    lives = [live_in(mine[d], capacity) for d in range(count)]
    reader, starts, _ = starts_of(lives, count)
    before = earlier_frames(tails_ref, period, periods, early)
    planes = []
    for row, part in enumerate(first_parts(*before, first_ref, first_core, width)):
        taps = [
            part[:, t * channels : (t + 1) * channels].reshape(HALO, width, channels)
            for t in range(TAPS)
        ]
        hidden = [
            taps[0][2] + taps[1][1] + taps[2][0],
            taps[0][3] + taps[1][2] + taps[2][1],
            head_ref[0, row] + taps[1][3] + taps[2][2],
            head_ref[1, row] + taps[2][3],
        ]
        planes.append(second_planes(jnp.stack(hidden), width))
    extra[HALO] = jnp.zeros(extra.shape[1:], extra.dtype)
    for row, part in enumerate(convolve(planes, second_ref[...])):
        now = part[:, :half].reshape(HALO, width, half)
        previous = part[:, channels : channels + half].reshape(HALO, width, half)
        oldest = part[:, half:channels].reshape(HALO, width, half)
        extra[0, row] = now[2] + previous[1] + oldest[0]
        extra[1, row] = now[3] + previous[2] + oldest[1]
        extra[2, row] = previous[3] + oldest[2]
        extra[3, row] = oldest[3]

    copies = []
    for d in range(count):
        block = mine[d][...].astype(jnp.float32)
        left = block[:, :, :half]
        right = block[:, :, half:]
        top = jnp.where(first_core, left, right).reshape(capacity, upper, width, half)
        bottom = jnp.where(first_core, right, left).reshape(capacity, upper, width, half)
        for k in range(capacity):
            at = starts[d] + k
            update = update_ref[at] + extra[jnp.minimum(at, HALO)]
            live = k < lives[d]
            for frame, low in ((top, 0), (bottom, upper)):
                value = frame[k] + update[low : low + upper]
                value = jnp.where(live, value, 0.0).astype(out_ref.dtype)
                out_ref[d * capacity + k, low : low + upper] = value
        source = out_ref.at[d * capacity : (d + 1) * capacity]
        target = out_hbm.at[pl.ds(reader[d] * capacity, capacity)]
        copies.append(pltpu.make_async_copy(source, target, sems.at[d]))
        copies[d].start()
    for copy in copies:
        copy.wait()


def call(kernel, out_shape, specs, scratch=(), flops=0, moved=0, mib=4, out_spec=VMEM):
    many = isinstance(out_shape, (list, tuple))
    return pl.pallas_call(
        kernel,
        out_shape=out_shape,
        in_specs=specs,
        out_specs=[out_spec] * len(out_shape) if many else out_spec,
        scratch_shapes=list(scratch),
        cost_estimate=pl.CostEstimate(flops=flops, bytes_accessed=moved, transcendentals=0),
        compiler_params=pltpu.CompilerParams(vmem_limit_bytes=mib << 20),
    )


def body(video, frame_owner, conv_first, conv_second):
    count = lax.axis_size("clips")
    periods = lax.axis_size("tm")
    local = video[0]
    slot_total, rows, width, half = local.shape
    capacity = max(2, 2 * slot_total // count)
    slots = count * capacity
    channels = 2 * half
    tile = (rows // 2 * width, channels)
    bf16 = jnp.bfloat16
    block = jax.ShapeDtypeStruct((capacity,) + tile, bf16)
    depth = TAPS * TAPS * channels

    hbm = pl.BlockSpec(memory_space=pltpu.HBM)
    taps = jax.ShapeDtypeStruct((TAPS, depth, channels), bf16)
    *packed, first, second = call(
        functools.partial(pack_kernel, count),
        [block] * count + [taps, taps],
        [hbm] * 4,
        [
            pltpu.SMEM((slot_total,), jnp.int32),
            pltpu.VMEM(local.shape, bf16),
            pltpu.VMEM((count, capacity) + tile, bf16),
            pltpu.SemaphoreType.DMA((PIECES + 3,)),
        ],
        moved=slots * half * rows * width * 4,
    )(
        *(
            pltpu.with_memory_space_constraint(a, pltpu.HBM)
            for a in (
                frame_owner[0, :, 0],
                local,
                conv_first.reshape(taps.shape),
                conv_second.reshape(taps.shape),
            )
        )
    )
    rounds = pairing(count)
    mine = [packed[0]] + [None] * (count - 1)
    for d in reversed(range(1, count)):
        mine[d] = lax.ppermute(packed[d], "clips", [(i, rounds[d][i]) for i in range(count)])
    second = call(
        half_weights_kernel,
        jax.ShapeDtypeStruct((depth, 2 * channels), bf16),
        [VMEM],
        moved=5 * depth * channels * 2,
    )(second)

    other = []
    for d in range(count):
        other.append(lax.ppermute(mine[d], "chan", [(0, 1), (1, 0)]))
    products = (rows, width, TAPS * channels)
    first_call = call(
        functools.partial(first_kernel, width),
        jax.ShapeDtypeStruct((capacity,) + products, jnp.float32),
        [VMEM] * 3,
        flops=2 * capacity * rows * width * depth * TAPS * channels,
        moved=4 * depth * channels * TAPS,
    )
    far = clip_rounds(count)
    fresh = far[1:]
    parts = {}
    for d in (0, far[0]):
        parts[d] = first_call(mine[d], other[d], first)
    tail = call(
        functools.partial(tail_kernel, count, capacity),
        jax.ShapeDtypeStruct((2, HALO) + tile, bf16),
        [VMEM] * (2 * count),
        [pltpu.VMEM((HALO + slots + 1,) + tile, bf16)] * 2,
        moved=slots * tile[0] * channels * 8,
    )(*mine, *other)
    if periods == 2:
        tails = lax.ppermute(tail, "tm", [(0, 1), (1, 0)])[None]
    else:
        tails = lax.all_gather(tail, "tm")
    update, head = call(
        functools.partial(middle_kernel, count, capacity, fresh),
        [
            jax.ShapeDtypeStruct((slots + capacity, rows, width, half), jnp.float32),
            jax.ShapeDtypeStruct((BACK, rows, width, channels), jnp.float32),
        ],
        [VMEM] * (2 * count + 2),
        [pltpu.VMEM((slots + 1,) + products, jnp.float32)],
        flops=2 * slots * rows * width * depth * TAPS * channels,
        moved=slots * tile[0] * channels * 8,
        mib=16,
    )(*mine, *(other[d] for d in fresh), *(parts[d] for d in sorted(parts)), first, second)
    out = call(
        functools.partial(last_kernel, count, capacity, periods),
        jax.ShapeDtypeStruct((slots, rows, width, half), bf16),
        [VMEM] * (count + 5),
        [
            pltpu.VMEM((2, HALO + 1) + tile, bf16),
            pltpu.VMEM((HALO + 1, rows, width, half), jnp.float32),
            pltpu.VMEM((slots, rows, width, half), bf16),
            pltpu.SemaphoreType.DMA((count,)),
        ],
        flops=2 * HALO * rows * width * depth * TAPS * channels,
        moved=slots * tile[0] * channels * 8,
        out_spec=hbm,
        mib=8,
    )(*mine, update, head, tails, first, second)
    return out[None]


def clip_rounds(count):
    return ROUNDS if count == len(ROUNDS) + 1 else tuple(reversed(range(1, count)))


def solution(mesh):
    placed = (
        P(("groups", "tm"), "clips", None, None, "chan"),
        P(("groups", "tm"), "clips", None),
        P(),
        P(),
    )

    return jax.shard_map(
        body,
        mesh=mesh,
        in_specs=placed,
        out_specs=P(("groups", "tm"), "clips", None, None, "chan"),
        check_vma=False,
    )
```

```python
import functools

import jax
import jax.numpy as jnp
from jax import lax
from jax.experimental import pallas as pl
from jax.experimental.pallas import tpu as pltpu
from jax.sharding import PartitionSpec as P


EPSILON = 1e-06
EMPTY = 64.0
FILLED = 32.0
TAPS = 3
BACK = TAPS - 1
HALO = 2 * BACK
PIECES = 2
WIDTH = 8
ROUNDS = (2, 3, 1)
ARRIVALS = (2, 1, 3)
VMEM = pl.BlockSpec(memory_space=pltpu.VMEM)
SMEM = pl.BlockSpec(memory_space=pltpu.SMEM)


def pairing(count):
    if count & (count - 1) == 0:
        return [[i ^ d for i in range(count)] for d in range(count)]
    return [[(d - i) % count for i in range(count)] for d in range(count)]


def partner_round(me, other, count):
    if count & (count - 1) == 0:
        return me ^ other
    return lax.rem(me + other, count)


def pack_kernel(count, owner_hbm, video_hbm, *rest):
    outs, (owner_ref, video_ref, slots, sems) = rest[:count], rest[count:]
    frames, rows, width, channels = video_ref.shape
    piece = frames // PIECES
    owner_copy = pltpu.make_async_copy(owner_hbm, owner_ref, sems.at[PIECES])
    owner_copy.start()
    video_copies = []
    for i in range(PIECES):
        at = slice(i * piece, (i + 1) * piece)
        video_copies.append(
            pltpu.make_async_copy(video_hbm.at[at], video_ref.at[at], sems.at[i])
        )
        video_copies[i].start()
    me = lax.axis_index("clips")
    first_core = lax.axis_index("chan") == 0
    half = rows // 2
    slots[...] = jnp.full(slots.shape, EMPTY, slots.dtype)
    owner_copy.wait()
    bits = 32 // count
    used = jnp.int32(0)
    for s in range(frames):
        if s % piece == 0:
            video_copies[s // piece].wait()
        o = owner_ref[s]
        k = lax.shift_right_logical(used, o * bits) & (2**bits - 1)
        used = used + lax.shift_left(jnp.int32(1), o * bits)
        upper = video_ref[s, :half].reshape(half * width, channels)
        lower = video_ref[s, half:].reshape(half * width, channels)
        left = jnp.where(first_core, upper, lower)
        right = jnp.where(first_core, lower, upper)
        slots[partner_round(me, o, count), k] = jnp.concatenate([left, right], axis=1)
    for d in range(count):
        outs[d][...] = slots[d]


def weights_kernel(raw_ref, out_ref):
    first_core = lax.axis_index("chan") == 0
    channels = raw_ref.shape[2]
    half = channels // 2

    def mine(t):
        full = raw_ref[t].astype(jnp.float32)
        return jnp.where(first_core, full[:, :half], full[:, half:])

    ahead = jnp.concatenate([mine(0), mine(2)], axis=1)
    out_ref[:, :channels] = ahead.astype(out_ref.dtype)
    behind = mine(1)
    out_ref[:, channels:] = jnp.concatenate([behind, behind], axis=1).astype(out_ref.dtype)


def filled(block, k):
    return (block[k, :8, :].astype(jnp.float32) < FILLED).astype(jnp.int32)


def live_in(block, capacity):
    total = filled(block, 0)
    for k in range(1, capacity):
        total = total + filled(block, k)
    return jnp.max(total)


def starts_of(lives, count):
    me = lax.axis_index("clips")
    reader = [partner_round(me, d, count) for d in range(count)]
    starts = []
    for d in range(count):
        start = jnp.int32(0)
        for e in range(count):
            if e != d:
                start = start + jnp.where(reader[e] < reader[d], lives[e], 0)
        starts.append(start)
    total = lives[0]
    for e in range(1, count):
        total = total + lives[e]
    return reader, starts, total


def tail_kernel(count, capacity, *rest):
    mine, other = rest[:count], rest[count : 2 * count]
    out_ref, mine_seq, other_seq = rest[2 * count :]
    lives = [live_in(mine[d], capacity) for d in range(count)]
    _, starts, total = starts_of(lives, count)
    dump = HALO + count * capacity
    for i in range(HALO):
        mine_seq[i] = jnp.full(mine_seq.shape[1:], EMPTY, mine_seq.dtype)
        other_seq[i] = jnp.full(mine_seq.shape[1:], EMPTY, mine_seq.dtype)
    for d in range(count):
        for k in range(capacity):
            place = jnp.where(k < lives[d], HALO + starts[d] + k, dump)
            mine_seq[place] = mine[d][k]
            other_seq[place] = other[d][k]
    for k in range(HALO):
        out_ref[0, k] = mine_seq[total + k]
        out_ref[1, k] = other_seq[total + k]


def activate(values):
    meansq = jnp.mean(values * values, axis=-1, keepdims=True)
    scaled = values * lax.rsqrt(meansq + EPSILON)
    return scaled / (1.0 + jnp.exp(-scaled))


def join_halves(mine, other, first_core):
    frames, tall, channels = mine.shape
    half = channels // 2
    width = WIDTH
    upper = tall // width
    lane_low = lax.broadcasted_iota(jnp.int32, mine.shape, 2) < half
    front = jnp.where(first_core, mine, other)
    back = jnp.where(first_core, other, mine)
    tops = jnp.where(lane_low, front, back).reshape(frames, upper, width, channels)
    bottoms = jnp.where(lane_low, back, front).reshape(frames * tall, channels)
    bottoms = pltpu.roll(bottoms, half, 1).reshape(frames, upper, width, channels)
    return [tops[:, i] for i in range(upper)] + [bottoms[:, i] for i in range(upper)]


def tap_planes(values, width):
    count = values.shape[0]
    column = lax.rem(lax.broadcasted_iota(jnp.int32, values.shape, 0), width)
    before = jnp.where(column == 0, 0.0, pltpu.roll(values, 1, 0))
    after = jnp.where(column == width - 1, 0.0, pltpu.roll(values, count - 1, 0))
    return jnp.concatenate([before, values, after], axis=1).astype(jnp.bfloat16)


def convolve(planes, weights):
    rows = len(planes)
    count = planes[0].shape[0]
    zero = jnp.zeros_like(planes[0])
    padded = [zero] + planes + [zero]
    stacked = jnp.concatenate(
        [jnp.concatenate(padded[row : row + TAPS], axis=1) for row in range(rows)], axis=0
    )
    out = jnp.dot(stacked, weights, preferred_element_type=jnp.float32)
    return [out[row * count : (row + 1) * count] for row in range(rows)]


def first_parts(mine, other, weights_ref, first_core, width):
    frames = mine.shape[0]
    values = join_halves(mine, other, first_core)
    channels = values[0].shape[2]
    planes = [
        tap_planes(activate(v.reshape(frames * width, channels)), width) for v in values
    ]
    weights = jnp.concatenate([weights_ref[t] for t in range(TAPS)], axis=1)
    return convolve(planes, weights)


def first_kernel(width, mine_ref, other_ref, weights_ref, out_ref):
    frames = mine_ref.shape[0]
    first_core = lax.axis_index("chan") == 0
    parts = first_parts(
        mine_ref[...].astype(jnp.float32),
        other_ref[...].astype(jnp.float32),
        weights_ref,
        first_core,
        width,
    )
    for row, part in enumerate(parts):
        out_ref[:, row] = part.reshape(frames, width, part.shape[1])


def earlier_frames(tails_ref, period, periods, scratch):
    if periods == 2:
        both = tails_ref[0].astype(jnp.float32)
        both = jnp.where((both < FILLED) & (period > 0), both, 0.0)
        return both[0], both[1]
    scratch[...] = jnp.zeros(scratch.shape, scratch.dtype)
    later = jnp.int32(0)
    for q in reversed(range(periods - 1)):
        live = jnp.max(filled(tails_ref.at[q, 0], 0))
        for k in range(1, HALO):
            live = live + jnp.max(filled(tails_ref.at[q, 0], k))
        live = jnp.where(q < period, live, 0)
        later = later + live
        for k in range(HALO):
            at = live - later + k
            place = jnp.where((k >= HALO - live) & (at >= 0), at, HALO)
            scratch[0, place] = tails_ref[q, 0, k]
            scratch[1, place] = tails_ref[q, 1, k]
    both = scratch[:, :HALO].astype(jnp.float32)
    return both[0], both[1]


def second_planes(hidden, width):
    frames, _, channels = hidden.shape
    hidden = hidden.reshape(frames * width, channels).astype(jnp.bfloat16).astype(jnp.float32)
    return tap_planes(activate(hidden), width)


def middle_kernel(count, capacity, fresh, *rest):
    mine, rest = rest[:count], rest[count:]
    ready = [d for d in range(count) if d != fresh]
    parts, rest = dict(zip(ready, rest[: len(ready)])), rest[len(ready) :]
    other_ref, first_ref, second_ref, head_ref, base_ref, out_hbm, *scratch = rest
    sequence, update_ref, out_ref, sems = scratch
    first_core = lax.axis_index("chan") == 0
    period = lax.axis_index("tm")
    slots = count * capacity
    _, rows, width, channels = head_ref.shape
    half = channels // 2

    lives = [live_in(mine[d], capacity) for d in range(count)]
    reader, starts, _ = starts_of(lives, count)

    def place(d, k):
        return jnp.where(k < lives[d], BACK + starts[d] + k, BACK + slots)

    sequence[:BACK] = jnp.zeros((BACK,) + sequence.shape[1:], sequence.dtype)
    for d in ready:
        for k in range(capacity):
            sequence[place(d, k)] = parts[d][k]
    own = mine[fresh][...].astype(jnp.float32)
    far = other_ref[...].astype(jnp.float32)
    for row, part in enumerate(first_parts(own, far, first_ref, first_core, width)):
        part = part.reshape(capacity, width, part.shape[1])
        for k in range(capacity):
            sequence[place(fresh, k), row] = part[k]

    planes = []
    for row in range(rows):
        hidden = sequence[BACK : BACK + slots, row, :, :channels]
        for t in range(1, TAPS):
            lanes = slice(t * channels, (t + 1) * channels)
            hidden = hidden + sequence[BACK - t : BACK - t + slots, row, :, lanes]
        head = hidden[:BACK]
        head_ref[:, row] = head
        head = jnp.where(period > 0, 0.0, head)
        planes.append(second_planes(jnp.concatenate([head, hidden[BACK:]], axis=0), width))
    zero = jnp.zeros((width, half), jnp.float32)
    for row, part in enumerate(convolve(planes, second_ref[...])):
        now = part[:, :half]
        previous = jnp.concatenate([zero, part[:-width, channels : channels + half]], axis=0)
        oldest = jnp.concatenate([zero, zero, part[: -2 * width, half:channels]], axis=0)
        at = slice(row * width, (row + 1) * width)
        update_ref[:slots, at] = (now + previous + oldest).reshape(slots, width, half)

    copies = []
    for d in range(count):
        block = mine[d][...].astype(jnp.float32)
        left = block[:, :, :half]
        right = block[:, :, half:]
        top = jnp.where(first_core, left, right)
        bottom = jnp.where(first_core, right, left)
        for k in range(capacity):
            at = starts[d] + k
            live = k < lives[d]
            value = jnp.concatenate([top[k], bottom[k]], axis=0) + update_ref[at]
            base_ref[jnp.where(live, jnp.minimum(at, HALO), HALO)] = value
            out_ref[d * capacity + k] = jnp.where(live, value, 0.0).astype(out_ref.dtype)
        source = out_ref.at[d * capacity : (d + 1) * capacity]
        target = out_hbm.at[pl.ds(reader[d] * capacity, capacity)]
        copies.append(pltpu.make_async_copy(source, target, sems.at[d]))
        copies[d].start()
    for copy in copies:
        copy.wait()


def last_kernel(count, capacity, periods, *rest):
    mine, rest = rest[:count], rest[count:]
    head_ref, base_ref, tails_ref, first_ref, second_ref, _, out_hbm, early, out_ref, sems = rest
    first_core = lax.axis_index("chan") == 0
    period = lax.axis_index("tm")
    _, _, width, channels = head_ref.shape
    half = channels // 2

    @pl.when(period > 0)
    def _():
        lives = [live_in(mine[d], capacity) for d in range(count)]
        reader, starts, total = starts_of(lives, count)
        before = earlier_frames(tails_ref, period, periods, early)
        planes = []
        for row, part in enumerate(first_parts(*before, first_ref, first_core, width)):
            taps = [
                part[:, t * channels : (t + 1) * channels].reshape(HALO, width, channels)
                for t in range(TAPS)
            ]
            hidden = [
                taps[0][2] + taps[1][1] + taps[2][0],
                taps[0][3] + taps[1][2] + taps[2][1],
                head_ref[0, row] + taps[1][3] + taps[2][2],
                head_ref[1, row] + taps[2][3],
            ]
            planes.append(second_planes(jnp.stack(hidden), width))
        for row, part in enumerate(convolve(planes, second_ref[...])):
            now = part[:, :half].reshape(HALO, width, half)
            previous = part[:, channels : channels + half].reshape(HALO, width, half)
            oldest = part[:, half:channels].reshape(HALO, width, half)
            extra = [
                now[2] + previous[1] + oldest[0],
                now[3] + previous[2] + oldest[1],
                previous[3] + oldest[2],
                oldest[3],
            ]
            at = slice(row * width, (row + 1) * width)
            value = base_ref[:HALO, at] + jnp.stack(extra)
            out_ref[:, at] = value.astype(out_ref.dtype)

        slots = []
        for i in range(HALO):
            slot = jnp.int32(0)
            for d in range(count):
                inside = (starts[d] <= i) & (i < starts[d] + lives[d])
                slot = slot + jnp.where(inside, reader[d] * capacity + i - starts[d], 0)
            slots.append(slot)
        for step in ("start", "wait"):
            for i in range(HALO):

                @pl.when(i < total)
                def _():
                    copy = pltpu.make_async_copy(out_ref.at[i], out_hbm.at[slots[i]], sems.at[i])
                    getattr(copy, step)()


def call(kernel, outs, specs, scratch=(), flops=0, moved=0, mib=4, out=None, alias=None):
    return pl.pallas_call(
        kernel,
        out_shape=outs,
        in_specs=specs,
        out_specs=out or jax.tree.map(lambda _: VMEM, outs),
        scratch_shapes=list(scratch),
        input_output_aliases=alias or {},
        cost_estimate=pl.CostEstimate(flops=flops, bytes_accessed=moved, transcendentals=0),
        compiler_params=pltpu.CompilerParams(vmem_limit_bytes=mib << 20),
    )


def body(video, frame_owner, conv_first, conv_second):
    count = lax.axis_size("clips")
    periods = lax.axis_size("tm")
    local = video[0]
    slot_total, rows, width, half = local.shape
    capacity = max(2, 2 * slot_total // count)
    slots = count * capacity
    channels = 2 * half
    tile = (rows // 2 * width, channels)
    bf16 = jnp.bfloat16
    block = jax.ShapeDtypeStruct((capacity,) + tile, bf16)
    depth = TAPS * TAPS * channels

    hbm = pl.BlockSpec(memory_space=pltpu.HBM)
    taps = jax.ShapeDtypeStruct((TAPS, depth, channels), bf16)
    packed = call(
        functools.partial(pack_kernel, count),
        [block] * count,
        [hbm] * 2,
        [
            pltpu.SMEM((slot_total,), jnp.int32),
            pltpu.VMEM(local.shape, bf16),
            pltpu.VMEM((count, capacity) + tile, bf16),
            pltpu.SemaphoreType.DMA((PIECES + 1,)),
        ],
        flops=2000000000,
        moved=slots * half * rows * width * 4,
    )(
        *(
            pltpu.with_memory_space_constraint(a, pltpu.HBM)
            for a in (
                frame_owner[0, :, 0],
                local,
            )
        )
    )
    rounds = pairing(count)
    mine = [packed[0]] + [None] * (count - 1)
    for d in reversed(range(1, count)):
        mine[d] = lax.ppermute(packed[d], "clips", [(i, rounds[d][i]) for i in range(count)])
    first = conv_first.reshape(taps.shape)
    second = call(
        weights_kernel,
        jax.ShapeDtypeStruct((depth, 2 * channels), bf16),
        [VMEM],
        moved=5 * depth * channels * 2,
    )(conv_second.reshape(taps.shape))
    other = []
    for d in range(count):
        other.append(lax.ppermute(mine[d], "chan", [(0, 1), (1, 0)]))
    products = (rows, width, TAPS * channels)
    first_call = call(
        functools.partial(first_kernel, width),
        jax.ShapeDtypeStruct((capacity,) + products, jnp.float32),
        [VMEM] * 3,
        flops=2 * capacity * rows * width * depth * TAPS * channels,
        moved=4 * depth * channels * TAPS,
    )
    arrivals = clip_rounds(count)[1]
    fresh = arrivals[-1]
    parts = {}
    for d in (0,) + arrivals[:-1]:
        parts[d] = first_call(mine[d], other[d], first)
    tail = call(
        functools.partial(tail_kernel, count, capacity),
        jax.ShapeDtypeStruct((2, HALO) + tile, bf16),
        [VMEM] * (2 * count),
        [pltpu.VMEM((HALO + slots + 1,) + tile, bf16)] * 2,
        moved=slots * tile[0] * channels * 8,
    )(*mine, *other)
    if periods == 2:
        tails = lax.ppermute(tail, "tm", [(0, 1), (1, 0)])[None]
    else:
        tails = lax.all_gather(tail, "tm")
    finished = jax.ShapeDtypeStruct((slots, rows * width, half), bf16)
    head, base, out = call(
        functools.partial(middle_kernel, count, capacity, fresh),
        [
            jax.ShapeDtypeStruct((BACK, rows, width, channels), jnp.float32),
            jax.ShapeDtypeStruct((HALO + 1, rows * width, half), jnp.float32),
            finished,
        ],
        [VMEM] * (2 * count + 2),
        [
            pltpu.VMEM((BACK + slots + 1,) + products, jnp.float32),
            pltpu.VMEM((slots + capacity, rows * width, half), jnp.float32),
            pltpu.VMEM(finished.shape, bf16),
            pltpu.SemaphoreType.DMA((count,)),
        ],
        flops=2 * slots * rows * width * depth * TAPS * channels,
        moved=slots * tile[0] * channels * 8,
        mib=16,
        out=[VMEM, VMEM, hbm],
    )(*mine, *(parts[d] for d in sorted(parts)), other[fresh], first, second)
    out = call(
        functools.partial(last_kernel, count, capacity, periods),
        finished,
        [VMEM] * (count + 5) + [hbm],
        [
            pltpu.VMEM((2, HALO + 1) + tile, bf16),
            pltpu.VMEM((HALO, rows * width, half), bf16),
            pltpu.SemaphoreType.DMA((HALO,)),
        ],
        flops=2 * HALO * rows * width * depth * TAPS * channels,
        moved=slots * tile[0] * channels * 8,
        mib=8,
        out=hbm,
        alias={count + 5: 0},
    )(*mine, head, base, tails, first, second, out)
    return out.reshape(1, slots, rows, width, half)


def clip_rounds(count):
    if count == len(ROUNDS) + 1:
        return ROUNDS, ARRIVALS
    far = tuple(reversed(range(1, count)))
    return far, far


def solution(mesh):
    placed = (
        P(("groups", "tm"), "clips", None, None, "chan"),
        P(("groups", "tm"), "clips", None),
        P(),
        P(),
    )

    return jax.shard_map(
        body,
        mesh=mesh,
        in_specs=placed,
        out_specs=P(("groups", "tm"), "clips", None, None, "chan"),
        check_vma=False,
    )
```

```python
import functools

import jax
import jax.numpy as jnp
from jax import lax
from jax.experimental import pallas as pl
from jax.experimental.pallas import tpu as pltpu
from jax.sharding import PartitionSpec as P


EPSILON = 1e-06
EMPTY = 64.0
FILLED = 32.0
TAPS = 3
BACK = TAPS - 1
HALO = 2 * BACK
PIECES = 4
WIDTH = 8
ROUNDS = (2, 3, 1)
ARRIVALS = (2, 1, 3)
VMEM = pl.BlockSpec(memory_space=pltpu.VMEM)
SMEM = pl.BlockSpec(memory_space=pltpu.SMEM)


def pairing(count):
    if count & (count - 1) == 0:
        return [[i ^ d for i in range(count)] for d in range(count)]
    return [[(d - i) % count for i in range(count)] for d in range(count)]


def partner_round(me, other, count):
    if count & (count - 1) == 0:
        return me ^ other
    return lax.rem(me + other, count)


def pack_kernel(count, owner_hbm, video_hbm, *rest):
    outs, (owner_ref, video_ref, slots, sems) = rest[:count], rest[count:]
    frames, rows, width, channels = video_ref.shape
    piece = frames // PIECES
    owner_copy = pltpu.make_async_copy(owner_hbm, owner_ref, sems.at[PIECES])
    owner_copy.start()
    video_copies = []
    for i in range(PIECES):
        at = slice(i * piece, (i + 1) * piece)
        video_copies.append(
            pltpu.make_async_copy(video_hbm.at[at], video_ref.at[at], sems.at[i])
        )
        video_copies[i].start()
    me = lax.axis_index("clips")
    first_core = lax.axis_index("chan") == 0
    half = rows // 2
    slots[...] = jnp.full(slots.shape, EMPTY, slots.dtype)
    owner_copy.wait()
    bits = 32 // count
    used = jnp.int32(0)
    for s in range(frames):
        if s % piece == 0:
            video_copies[s // piece].wait()
        o = owner_ref[s]
        k = lax.shift_right_logical(used, o * bits) & (2**bits - 1)
        used = used + lax.shift_left(jnp.int32(1), o * bits)
        upper = video_ref[s, :half].reshape(half * width, channels)
        lower = video_ref[s, half:].reshape(half * width, channels)
        left = jnp.where(first_core, upper, lower)
        right = jnp.where(first_core, lower, upper)
        slots[partner_round(me, o, count), k] = jnp.concatenate([left, right], axis=1)
    for d in range(count):
        outs[d][...] = slots[d]


def weights_kernel(raw_ref, out_ref):
    first_core = lax.axis_index("chan") == 0
    channels = raw_ref.shape[2]
    half = channels // 2

    def mine(t):
        full = raw_ref[t].astype(jnp.float32)
        return jnp.where(first_core, full[:, :half], full[:, half:])

    ahead = jnp.concatenate([mine(0), mine(2)], axis=1)
    out_ref[:, :channels] = ahead.astype(out_ref.dtype)
    behind = mine(1)
    out_ref[:, channels:] = jnp.concatenate([behind, behind], axis=1).astype(out_ref.dtype)


def filled(block, k):
    return (block[k, :8, :].astype(jnp.float32) < FILLED).astype(jnp.int32)


def live_in(block, capacity):
    total = filled(block, 0)
    for k in range(1, capacity):
        total = total + filled(block, k)
    return jnp.max(total)


def starts_of(lives, count):
    me = lax.axis_index("clips")
    reader = [partner_round(me, d, count) for d in range(count)]
    starts = []
    for d in range(count):
        start = jnp.int32(0)
        for e in range(count):
            if e != d:
                start = start + jnp.where(reader[e] < reader[d], lives[e], 0)
        starts.append(start)
    total = lives[0]
    for e in range(1, count):
        total = total + lives[e]
    return reader, starts, total


def tail_kernel(count, capacity, *rest):
    mine, other = rest[:count], rest[count : 2 * count]
    out_ref, mine_seq, other_seq = rest[2 * count :]
    lives = [live_in(mine[d], capacity) for d in range(count)]
    _, starts, total = starts_of(lives, count)
    dump = HALO + count * capacity
    for i in range(HALO):
        mine_seq[i] = jnp.full(mine_seq.shape[1:], EMPTY, mine_seq.dtype)
        other_seq[i] = jnp.full(mine_seq.shape[1:], EMPTY, mine_seq.dtype)
    for d in range(count):
        for k in range(capacity):
            place = jnp.where(k < lives[d], HALO + starts[d] + k, dump)
            mine_seq[place] = mine[d][k]
            other_seq[place] = other[d][k]
    for k in range(HALO):
        out_ref[0, k] = mine_seq[total + k]
        out_ref[1, k] = other_seq[total + k]


def activate(values):
    meansq = jnp.mean(values * values, axis=-1, keepdims=True)
    scaled = values * lax.rsqrt(meansq + EPSILON)
    return scaled / (1.0 + jnp.exp(-scaled))


def join_halves(mine, other, first_core):
    frames, tall, channels = mine.shape
    half = channels // 2
    width = WIDTH
    upper = tall // width
    lane_low = lax.broadcasted_iota(jnp.int32, mine.shape, 2) < half
    front = jnp.where(first_core, mine, other)
    back = jnp.where(first_core, other, mine)
    tops = jnp.where(lane_low, front, back).reshape(frames, upper, width, channels)
    bottoms = jnp.where(lane_low, back, front).reshape(frames * tall, channels)
    bottoms = pltpu.roll(bottoms, half, 1).reshape(frames, upper, width, channels)
    return [tops[:, i] for i in range(upper)] + [bottoms[:, i] for i in range(upper)]


def tap_planes(values, width):
    count = values.shape[0]
    column = lax.rem(lax.broadcasted_iota(jnp.int32, values.shape, 0), width)
    before = jnp.where(column == 0, 0.0, pltpu.roll(values, 1, 0))
    after = jnp.where(column == width - 1, 0.0, pltpu.roll(values, count - 1, 0))
    return jnp.concatenate([before, values, after], axis=1).astype(jnp.bfloat16)


def convolve(planes, weights):
    rows = len(planes)
    count = planes[0].shape[0]
    zero = jnp.zeros_like(planes[0])
    padded = [zero] + planes + [zero]
    stacked = jnp.concatenate(
        [jnp.concatenate(padded[row : row + TAPS], axis=1) for row in range(rows)], axis=0
    )
    out = jnp.dot(stacked, weights, preferred_element_type=jnp.float32)
    return [out[row * count : (row + 1) * count] for row in range(rows)]


def first_parts(mine, other, weights_ref, first_core, width):
    frames = mine.shape[0]
    values = join_halves(mine, other, first_core)
    channels = values[0].shape[2]
    planes = [
        tap_planes(activate(v.reshape(frames * width, channels)), width) for v in values
    ]
    weights = jnp.concatenate([weights_ref[t] for t in range(TAPS)], axis=1)
    return convolve(planes, weights)


def first_kernel(width, mine_ref, other_ref, weights_ref, out_ref):
    frames = mine_ref.shape[0]
    first_core = lax.axis_index("chan") == 0
    parts = first_parts(
        mine_ref[...].astype(jnp.float32),
        other_ref[...].astype(jnp.float32),
        weights_ref,
        first_core,
        width,
    )
    for row, part in enumerate(parts):
        out_ref[:, row] = part.reshape(frames, width, part.shape[1])


def earlier_frames(tails_ref, period, periods, scratch):
    if periods == 2:
        both = tails_ref[0].astype(jnp.float32)
        both = jnp.where((both < FILLED) & (period > 0), both, 0.0)
        return both[0], both[1]
    scratch[...] = jnp.zeros(scratch.shape, scratch.dtype)
    later = jnp.int32(0)
    for q in reversed(range(periods - 1)):
        live = jnp.max(filled(tails_ref.at[q, 0], 0))
        for k in range(1, HALO):
            live = live + jnp.max(filled(tails_ref.at[q, 0], k))
        live = jnp.where(q < period, live, 0)
        later = later + live
        for k in range(HALO):
            at = live - later + k
            place = jnp.where((k >= HALO - live) & (at >= 0), at, HALO)
            scratch[0, place] = tails_ref[q, 0, k]
            scratch[1, place] = tails_ref[q, 1, k]
    both = scratch[:, :HALO].astype(jnp.float32)
    return both[0], both[1]


def second_planes(hidden, width):
    frames, _, channels = hidden.shape
    hidden = hidden.reshape(frames * width, channels).astype(jnp.bfloat16).astype(jnp.float32)
    return tap_planes(activate(hidden), width)


def middle_kernel(count, capacity, fresh, *rest):
    mine, rest = rest[:count], rest[count:]
    ready = [d for d in range(count) if d != fresh]
    parts, rest = dict(zip(ready, rest[: len(ready)])), rest[len(ready) :]
    other_ref, first_ref, second_ref, head_ref, base_ref, out_hbm, *scratch = rest
    sequence, update_ref, out_ref, sems = scratch
    first_core = lax.axis_index("chan") == 0
    period = lax.axis_index("tm")
    slots = count * capacity
    _, rows, width, channels = head_ref.shape
    half = channels // 2

    lives = [live_in(mine[d], capacity) for d in range(count)]
    reader, starts, _ = starts_of(lives, count)

    def place(d, k):
        return jnp.where(k < lives[d], BACK + starts[d] + k, BACK + slots)

    sequence[:BACK] = jnp.zeros((BACK,) + sequence.shape[1:], sequence.dtype)
    for d in ready:
        for k in range(capacity):
            sequence[place(d, k)] = parts[d][k]
    own = mine[fresh][...].astype(jnp.float32)
    far = other_ref[...].astype(jnp.float32)
    for row, part in enumerate(first_parts(own, far, first_ref, first_core, width)):
        part = part.reshape(capacity, width, part.shape[1])
        for k in range(capacity):
            sequence[place(fresh, k), row] = part[k]

    planes = []
    for row in range(rows):
        hidden = sequence[BACK : BACK + slots, row, :, :channels]
        for t in range(1, TAPS):
            lanes = slice(t * channels, (t + 1) * channels)
            hidden = hidden + sequence[BACK - t : BACK - t + slots, row, :, lanes]
        head = hidden[:BACK]
        head_ref[:, row] = head
        head = jnp.where(period > 0, 0.0, head)
        planes.append(second_planes(jnp.concatenate([head, hidden[BACK:]], axis=0), width))
    zero = jnp.zeros((width, half), jnp.float32)
    for row, part in enumerate(convolve(planes, second_ref[...])):
        now = part[:, :half]
        previous = jnp.concatenate([zero, part[:-width, channels : channels + half]], axis=0)
        oldest = jnp.concatenate([zero, zero, part[: -2 * width, half:channels]], axis=0)
        at = slice(row * width, (row + 1) * width)
        update_ref[:slots, at] = (now + previous + oldest).reshape(slots, width, half)

    base_ref[...] = update_ref[:HALO]

    copies = []
    for d in range(count):
        block = mine[d][...].astype(jnp.float32)
        left = block[:, :, :half]
        right = block[:, :, half:]
        top = jnp.where(first_core, left, right)
        bottom = jnp.where(first_core, right, left)
        for k in range(capacity):
            at = starts[d] + k
            live = k < lives[d]
            value = jnp.concatenate([top[k], bottom[k]], axis=0) + update_ref[at]
            out_ref[d * capacity + k] = jnp.where(live, value, 0.0).astype(out_ref.dtype)
        source = out_ref.at[d * capacity : (d + 1) * capacity]
        target = out_hbm.at[pl.ds(reader[d] * capacity, capacity)]
        copies.append(pltpu.make_async_copy(source, target, sems.at[d]))
        copies[d].start()
    for copy in copies:
        copy.wait()


def last_kernel(count, capacity, periods, *rest):
    mine, rest = rest[:count], rest[count:]
    head_ref, base_ref, tails_ref, first_ref, second_ref, _, out_hbm, early, out_ref, sems = rest
    first_core = lax.axis_index("chan") == 0
    period = lax.axis_index("tm")
    _, _, width, channels = head_ref.shape
    half = channels // 2

    @pl.when(period > 0)
    def _():
        lives = [live_in(mine[d], capacity) for d in range(count)]
        reader, starts, total = starts_of(lives, count)
        frames = []
        for i in range(HALO):
            frame = mine[0][0]
            for d in range(count):
                k = i - starts[d]
                inside = (k >= 0) & (k < lives[d])
                frame = jnp.where(inside, mine[d][jnp.clip(k, 0, capacity - 1)], frame)
            frames.append(frame)
        frames = jnp.stack(frames).astype(jnp.float32)
        left = frames[:, :, :half]
        right = frames[:, :, half:]
        frames = jnp.concatenate(
            [jnp.where(first_core, left, right), jnp.where(first_core, right, left)], axis=1
        )
        before = earlier_frames(tails_ref, period, periods, early)
        planes = []
        for row, part in enumerate(first_parts(*before, first_ref, first_core, width)):
            taps = [
                part[:, t * channels : (t + 1) * channels].reshape(HALO, width, channels)
                for t in range(TAPS)
            ]
            hidden = [
                taps[0][2] + taps[1][1] + taps[2][0],
                taps[0][3] + taps[1][2] + taps[2][1],
                head_ref[0, row] + taps[1][3] + taps[2][2],
                head_ref[1, row] + taps[2][3],
            ]
            planes.append(second_planes(jnp.stack(hidden), width))
        for row, part in enumerate(convolve(planes, second_ref[...])):
            now = part[:, :half].reshape(HALO, width, half)
            previous = part[:, channels : channels + half].reshape(HALO, width, half)
            oldest = part[:, half:channels].reshape(HALO, width, half)
            extra = [
                now[2] + previous[1] + oldest[0],
                now[3] + previous[2] + oldest[1],
                previous[3] + oldest[2],
                oldest[3],
            ]
            at = slice(row * width, (row + 1) * width)
            value = frames[:, at] + base_ref[:, at] + jnp.stack(extra)
            out_ref[:, at] = value.astype(out_ref.dtype)

        slots = []
        for i in range(HALO):
            slot = jnp.int32(0)
            for d in range(count):
                inside = (starts[d] <= i) & (i < starts[d] + lives[d])
                slot = slot + jnp.where(inside, reader[d] * capacity + i - starts[d], 0)
            slots.append(slot)
        for step in ("start", "wait"):
            for i in range(HALO):

                @pl.when(i < total)
                def _():
                    copy = pltpu.make_async_copy(out_ref.at[i], out_hbm.at[slots[i]], sems.at[i])
                    getattr(copy, step)()


def call(kernel, outs, specs, scratch=(), flops=0, moved=0, mib=4, out=None, alias=None):
    return pl.pallas_call(
        kernel,
        out_shape=outs,
        in_specs=specs,
        out_specs=out or jax.tree.map(lambda _: VMEM, outs),
        scratch_shapes=list(scratch),
        input_output_aliases=alias or {},
        cost_estimate=pl.CostEstimate(flops=flops, bytes_accessed=moved, transcendentals=0),
        compiler_params=pltpu.CompilerParams(vmem_limit_bytes=mib << 20),
    )


def body(video, frame_owner, conv_first, conv_second):
    count = lax.axis_size("clips")
    periods = lax.axis_size("tm")
    local = video[0]
    slot_total, rows, width, half = local.shape
    capacity = max(2, 2 * slot_total // count)
    slots = count * capacity
    channels = 2 * half
    tile = (rows // 2 * width, channels)
    bf16 = jnp.bfloat16
    block = jax.ShapeDtypeStruct((capacity,) + tile, bf16)
    depth = TAPS * TAPS * channels

    hbm = pl.BlockSpec(memory_space=pltpu.HBM)
    taps = jax.ShapeDtypeStruct((TAPS, depth, channels), bf16)
    packed = call(
        functools.partial(pack_kernel, count),
        [block] * count,
        [hbm] * 2,
        [
            pltpu.SMEM((slot_total,), jnp.int32),
            pltpu.VMEM(local.shape, bf16),
            pltpu.VMEM((count, capacity) + tile, bf16),
            pltpu.SemaphoreType.DMA((PIECES + 1,)),
        ],
        flops=2000000000,
        moved=slots * half * rows * width * 4,
    )(
        *(
            pltpu.with_memory_space_constraint(a, pltpu.HBM)
            for a in (
                frame_owner[0, :, 0],
                local,
            )
        )
    )
    rounds = pairing(count)
    mine = [packed[0]] + [None] * (count - 1)
    for d in reversed(range(1, count)):
        mine[d] = lax.ppermute(packed[d], "clips", [(i, rounds[d][i]) for i in range(count)])
    first = conv_first.reshape(taps.shape)
    second = call(
        weights_kernel,
        jax.ShapeDtypeStruct((depth, 2 * channels), bf16),
        [VMEM],
        moved=5 * depth * channels * 2,
    )(conv_second.reshape(taps.shape))
    other = []
    for d in range(count):
        other.append(lax.ppermute(mine[d], "chan", [(0, 1), (1, 0)]))
    products = (rows, width, TAPS * channels)
    first_call = call(
        functools.partial(first_kernel, width),
        jax.ShapeDtypeStruct((capacity,) + products, jnp.float32),
        [VMEM] * 3,
        flops=2 * capacity * rows * width * depth * TAPS * channels,
        moved=4 * depth * channels * TAPS,
    )
    arrivals = clip_rounds(count)[1]
    fresh = arrivals[-1]
    parts = {}
    for d in (0,) + arrivals[:-1]:
        parts[d] = first_call(mine[d], other[d], first)
    tail = call(
        functools.partial(tail_kernel, count, capacity),
        jax.ShapeDtypeStruct((2, HALO) + tile, bf16),
        [VMEM] * (2 * count),
        [pltpu.VMEM((HALO + slots + 1,) + tile, bf16)] * 2,
        moved=slots * tile[0] * channels * 8,
    )(*mine, *other)
    if periods == 2:
        tails = lax.ppermute(tail, "tm", [(0, 1), (1, 0)])[None]
    else:
        tails = lax.all_gather(tail, "tm")
    finished = jax.ShapeDtypeStruct((slots, rows * width, half), bf16)
    head, base, out = call(
        functools.partial(middle_kernel, count, capacity, fresh),
        [
            jax.ShapeDtypeStruct((BACK, rows, width, channels), jnp.float32),
            jax.ShapeDtypeStruct((HALO, rows * width, half), jnp.float32),
            finished,
        ],
        [VMEM] * (2 * count + 2),
        [
            pltpu.VMEM((BACK + slots + 1,) + products, jnp.float32),
            pltpu.VMEM((slots + capacity, rows * width, half), jnp.float32),
            pltpu.VMEM(finished.shape, bf16),
            pltpu.SemaphoreType.DMA((count,)),
        ],
        flops=2 * slots * rows * width * depth * TAPS * channels,
        moved=slots * tile[0] * channels * 8,
        mib=16,
        out=[VMEM, VMEM, hbm],
    )(*mine, *(parts[d] for d in sorted(parts)), other[fresh], first, second)
    out = call(
        functools.partial(last_kernel, count, capacity, periods),
        finished,
        [VMEM] * (count + 5) + [hbm],
        [
            pltpu.VMEM((2, HALO + 1) + tile, bf16),
            pltpu.VMEM((HALO, rows * width, half), bf16),
            pltpu.SemaphoreType.DMA((HALO,)),
        ],
        flops=2 * HALO * rows * width * depth * TAPS * channels,
        moved=slots * tile[0] * channels * 8,
        mib=8,
        out=hbm,
        alias={count + 5: 0},
    )(*mine, head, base, tails, first, second, out)
    return out.reshape(1, slots, rows, width, half)


def clip_rounds(count):
    if count == len(ROUNDS) + 1:
        return ROUNDS, ARRIVALS
    far = tuple(reversed(range(1, count)))
    return far, far


def solution(mesh):
    placed = (
        P(("groups", "tm"), "clips", None, None, "chan"),
        P(("groups", "tm"), "clips", None),
        P(),
        P(),
    )

    return jax.shard_map(
        body,
        mesh=mesh,
        in_specs=placed,
        out_specs=P(("groups", "tm"), "clips", None, None, "chan"),
        check_vma=False,
    )
```
